1024 devices in a mesh: seq: 128 (over y, x, core), head: 8 (over z).
Axes of the slice: x: 8, y: 8, z: 8, core: 2. Of those that a mesh axis runs over, the one named last changes fastest.
Arguments:
- queries: bfloat16 [1, 163840, 2048], P(None, ('seq', 'head')), may hold values from -6 to 6
- keys: bfloat16 [1, 163840, 2048], P(None, ('seq', 'head')), may hold values from -6 to 6
- values: bfloat16 [1, 163840, 2048], P(None, ('seq', 'head')), may hold values from -6 to 6
- decay_exp: int32 [16], replicated, may hold values from 0 to 11
- norm_gain: float32 [2048], P('head'), may hold values from 0.5 to 1.5
Outputs:
- attended: bfloat16 [1, 163840, 2048], P(None, 'seq', 'head')
The draws below stay inside these ranges and needn't reach their ends.
All inputs are finite; a program needn't handle non-finite values.
Results may differ from the reference program's by a relative error of at most 0.0059.
Values may be sent and summed in bfloat16 or wider, within the bound.
A program may use at most 64 MiB of HBM per device.

```python
import jax
import jax.numpy as jnp
from jax import lax

HEADS = 16
DH = 128
BLOCK = 128
BATCH = 1
TOKENS = 163840


def plant(values, key, smallest, largest):
    shape = values.shape
    index_at = [jax.random.randint(jax.random.fold_in(key, axis), (), 0, shape[axis]) for axis in range(len(shape))]
    values = values.at[tuple(index_at)].set(smallest)
    longest = shape.index(max(shape))
    index_at[longest] = (index_at[longest] + 1) % shape[longest]
    return values.at[tuple(index_at)].set(largest)


def steps_of(stream_key, dims, split, low, high):
    level, own = 1.0, jax.random.fold_in(stream_key, 6)
    for position, blocks in split:
        steps = jnp.exp(jax.random.uniform(jax.random.fold_in(own, position), (blocks,), jnp.float32, low / len(split), high / len(split)))
        level = level * jnp.repeat(steps, dims[position] // blocks).reshape([-1 if axis == position else 1 for axis in range(len(dims))])
    return level


def bell_draw(stream_key, extent, width, most, split=(), kind=jnp.bfloat16):
    values = jax.random.normal(stream_key, extent, jnp.float32) * width
    if len(split) > 0:
        values = steps_of(stream_key, extent, split, -0.22, 0.18) * values
    return jnp.clip(values, min=-most, max=most).astype(kind)


def setup_inputs(seed: int = 0) -> dict:
    arg_keys = jax.random.split(jax.random.key(seed), 6)
    return {
        "queries": bell_draw(arg_keys[0], (BATCH, TOKENS, HEADS * DH), 1.0, 6.0, ((1, 1024),)),
        "keys": bell_draw(arg_keys[1], (BATCH, TOKENS, HEADS * DH), 1.0, 6.0, ((1, 1024),)),
        "values": bell_draw(arg_keys[2], (BATCH, TOKENS, HEADS * DH), 1.0, 6.0, ((1, 1024),)),
        "decay_exp": plant(jax.random.randint(arg_keys[3], (HEADS,), 0, 12), jax.random.fold_in(arg_keys[3], 1), 0, 11).astype(jnp.int32),
        "norm_gain": jnp.clip(1.0 + 0.1 * jax.random.normal(arg_keys[4], (HEADS * DH,), jnp.float32), 0.5, 1.5),
    }


def reference(queries, keys, values, decay_exp, norm_gain):
    f32 = jnp.float32
    bf16 = jnp.bfloat16
    rate = jnp.exp2(decay_exp.astype(f32)) / (2.0 * TOKENS)
    batch = queries.shape[0]
    nblk = TOKENS // BLOCK

    def blocks(arr):
        return jnp.moveaxis(arr.reshape(batch, nblk, BLOCK, HEADS, DH), 1, 0)
    pos = jnp.arange(BLOCK).astype(f32)
    diff = pos[:, None] - pos[None, :]
    mask = jnp.where(diff >= 0, jnp.exp(-rate[:, None, None] * jnp.maximum(diff, 0.0)), 0.0)
    kfac = jnp.exp(-rate[None, :] * (BLOCK - 1 - pos)[:, None])
    qfac = jnp.exp(-rate[None, :] * (pos + 1.0)[:, None])
    step_decay = jnp.exp(-rate * BLOCK)
    gain = norm_gain.reshape(HEADS, DH)

    def step(state, xs):
        qb, kb, vb = xs
        qf = qb.astype(f32)
        kf = kb.astype(f32)
        vf = vb.astype(f32)
        scores = jnp.einsum('bihd,bjhd->bhij', qf, kf)
        probs = lax.optimization_barrier((scores * mask[None]).astype(bf16)).astype(f32)
        intra = jnp.einsum('bhij,bjhd->bihd', probs, vf)
        qdec = lax.optimization_barrier((qf * qfac[None, :, :, None]).astype(bf16)).astype(f32)
        kdec = lax.optimization_barrier((kf * kfac[None, :, :, None]).astype(bf16)).astype(f32)
        snap = lax.optimization_barrier(state.astype(bf16)).astype(f32)
        inter = jnp.einsum('bihd,bhde->bihe', qdec, snap)
        piece = jnp.einsum('bjhd,bjhe->bhde', kdec, vf)
        fresh = state * step_decay[None, :, None, None] + piece
        out = intra + inter
        scale = lax.rsqrt(lax.optimization_barrier(jnp.mean(out * out, axis=-1, keepdims=True)) + 1e-05)
        return (fresh, (out * scale * gain[None, None]).astype(bf16))
    start = jnp.zeros((batch, HEADS, DH, DH), f32)
    final, outs = lax.scan(step, start, (blocks(queries), blocks(keys), blocks(values)))
    return jnp.moveaxis(outs, 0, 1).reshape(batch, TOKENS, HEADS * DH)
```

```python
import functools

import jax
import jax.numpy as jnp
from jax import lax
from jax.experimental import pallas as pl
from jax.experimental.pallas import tpu as pltpu
from jax.sharding import PartitionSpec as P

HEADS = 16
DH = 128
BLOCK = 128
NX = 8
CORES = 2
MESH = pl.DeviceIdType.MESH
F32 = jnp.float32
BF16 = jnp.bfloat16


def power_of_two(e):
    r = jnp.float32(1.0)
    for bit in range(4):
        r = r * jnp.where((e >> bit) & 1 == 1, jnp.float32(2.0 ** (2**bit)), jnp.float32(1.0))
    return r


def nt(a, b):
    return lax.dot_general(a, b, (((1,), (1,)), ((), ())), preferred_element_type=F32)


def tn(a, b):
    return lax.dot_general(a, b, (((0,), (0,)), ((), ())), preferred_element_type=F32)


def nn(a, b):
    return jnp.dot(a, b, preferred_element_type=F32)


def kernel(
    n_z,
    n_y,
    total,
    q_hbm,
    k_hbm,
    v_hbm,
    dec_ref,
    gain_ref,
    out_ref,
    qb,
    kb,
    vb,
    before,
    intra,
    mask,
    kfac,
    qfac,
    gbuf,
    pair_in,
    xbuf,
    ybuf,
    last_out,
    last_in,
    local_sem,
    z_send,
    z_recv,
    x_send,
    x_recv,
    y_send,
    y_recv,
    p_send,
    p_recv,
):
    s = lax.axis_index("seq")
    z = lax.axis_index("head")
    core = lax.rem(s, CORES)
    x = lax.rem(lax.div(s, CORES), NX)
    y = lax.div(s, CORES * NX)
    part = q_hbm.shape[0]
    wide = q_hbm.shape[1] // n_z
    length = part * n_z
    nblk = length // BLOCK
    heads_here = wide // DH

    def seq_of(yy, xx, cc):
        return (yy * NX + xx) * CORES + cc

    def at_z(d):
        return (s, lax.rem(z + d, n_z))

    def at_x(d):
        return (seq_of(y, lax.rem(x + d, NX), core), z)

    def at_y(d):
        return (seq_of(lax.rem(y + d, n_y), x, core), z)

    partner = (seq_of(y, x, 1 - core), z)

    hbm = (k_hbm, v_hbm, q_hbm)
    vmem = (kb, vb, qb)
    own_cols = pl.ds(pl.multiple_of(z * wide, wide), wide)
    own_rows = pl.ds(pl.multiple_of(z * part, part), part)
    locals_ = []
    for a in range(3):
        copy = pltpu.make_async_copy(hbm[a].at[:, own_cols], vmem[a].at[own_rows], local_sem.at[a])
        copy.start()
        locals_.append(copy)

    barrier = pltpu.get_barrier_semaphore()
    for d in range(1, n_z):
        pl.semaphore_signal(barrier, inc=1, device_id=at_z(d), device_id_type=MESH)
    for d in range(1, NX):
        pl.semaphore_signal(barrier, inc=1, device_id=at_x(d), device_id_type=MESH)
    for d in range(1, n_y):
        pl.semaphore_signal(barrier, inc=1, device_id=at_y(d), device_id_type=MESH)
    pl.semaphore_signal(barrier, inc=1, device_id=partner, device_id_type=MESH)
    pl.semaphore_wait(barrier, n_z + NX + n_y - 2)

    order = sorted(range(1, n_z), key=lambda d: (-min(d, n_z - d), d))
    z_copies = []
    for a in range(3):
        copies = []
        for d in order:
            to = lax.rem(z + d, n_z)
            copy = pltpu.make_async_remote_copy(
                src_ref=hbm[a].at[:, pl.ds(pl.multiple_of(to * wide, wide), wide)],
                dst_ref=vmem[a].at[own_rows],
                send_sem=z_send.at[a, d],
                recv_sem=z_recv.at[a, d],
                device_id=(s, to),
                device_id_type=MESH,
            )
            copy.start()
            copies.append(copy)
        z_copies.append(copies)

    row = lax.broadcasted_iota(jnp.int32, (BLOCK, BLOCK), 0).astype(F32)
    col = lax.broadcasted_iota(jnp.int32, (BLOCK, BLOCK), 1).astype(F32)
    diff = row - col
    rates = []
    for h in range(heads_here):
        rate = power_of_two(dec_ref[z * heads_here + h]) / jnp.float32(2.0 * total)
        rates.append(rate)
        mask[h] = jnp.where(diff >= 0, jnp.exp(-rate * jnp.maximum(diff, 0.0)), 0.0)
        kfac[h] = jnp.exp(-rate * (BLOCK - 1 - row))
        qfac[h] = jnp.exp(-rate * (row + 1.0))
    rate_here = jnp.where(core == 0, rates[0], rates[1])

    def decay(rate, tokens):
        return jnp.exp(jnp.full((1, DH), -rate * tokens, F32))

    for a in (0, 1):
        locals_[a].wait()
        for copy in z_copies[a]:
            copy.wait_recv()

    step_decay = [decay(rates[h], BLOCK) for h in range(heads_here)]

    def state_step(b, states):
        rows = pl.ds(pl.multiple_of(b * BLOCK, BLOCK), BLOCK)
        fresh = []
        for h in range(heads_here):
            cols = slice(h * DH, (h + 1) * DH)
            before[h, b] = states[h]
            kdec = (kb[rows, cols].astype(F32) * kfac[h]).astype(BF16)
            fresh.append(states[h] * step_decay[h] + tn(kdec, vb[rows, cols]))
        return tuple(fresh)

    zero = jnp.zeros((DH, DH), F32)
    group = lax.fori_loop(0, nblk, state_step, (zero,) * heads_here)
    for h in range(heads_here):
        gbuf[h] = group[h]

    pair = pltpu.make_async_remote_copy(
        src_ref=gbuf.at[1 - core],
        dst_ref=pair_in,
        send_sem=p_send.at[0],
        recv_sem=p_recv.at[0],
        device_id=partner,
        device_id_type=MESH,
    )
    pair.start()
    w1 = decay(rate_here, length)
    pair.wait_recv()
    mine = gbuf[core]
    theirs = pair_in[...]
    first = jnp.where(core == 0, mine, theirs)
    second = jnp.where(core == 0, theirs, mine)
    xbuf[x] = (first * w1 + second).astype(BF16)
    x_copies = []
    for d in range(1, NX):
        copy = pltpu.make_async_remote_copy(
            src_ref=xbuf.at[x],
            dst_ref=xbuf.at[x],
            send_sem=x_send.at[d],
            recv_sem=x_recv.at[d],
            device_id=at_x(d),
            device_id_type=MESH,
        )
        copy.start()
        x_copies.append(copy)
    for copy in x_copies:
        copy.wait_recv()
    chip = CORES * length
    in_row = jnp.zeros((DH, DH), F32)
    row_total = jnp.zeros((DH, DH), F32)
    for i in range(NX):
        state = xbuf[i].astype(F32)
        gap = jnp.maximum(x - 1 - i, 0).astype(F32)
        in_row += state * jnp.where(i < x, decay(rate_here, chip * gap), 0.0)
        row_total += state * decay(rate_here, chip * (NX - 1.0 - i))
    ybuf[y] = row_total.astype(BF16)

    def y_copy(d):
        return pltpu.make_async_remote_copy(
            src_ref=ybuf.at[y],
            dst_ref=ybuf.at[y],
            send_sem=y_send.at[d],
            recv_sem=y_recv.at[d],
            device_id=at_y(d),
            device_id_type=MESH,
        )

    for d in range(1, n_y):
        y_copy(d).start()

    locals_[2].wait()
    for copy in z_copies[2]:
        copy.wait_recv()

    def intra_step(b, carry):
        rows = pl.ds(pl.multiple_of(b * BLOCK, BLOCK), BLOCK)
        for h in range(heads_here):
            cols = slice(h * DH, (h + 1) * DH)
            probs = (nt(qb[rows, cols], kb[rows, cols]) * mask[h]).astype(BF16)
            intra[rows, cols] = nn(probs, vb[rows, cols])
        return carry

    lax.fori_loop(0, nblk, intra_step, 0)

    for d in range(1, n_y):
        y_copy(d).wait_recv()
    above = jnp.zeros((DH, DH), F32)
    for i in range(n_y):
        gap = jnp.maximum(y - 1 - i, 0).astype(F32)
        above += ybuf[i].astype(F32) * jnp.where(i < y, decay(rate_here, chip * NX * gap), 0.0)
    incoming = above * decay(rate_here, chip * x.astype(F32)) + in_row
    after = incoming * w1 + first
    last_out[...] = jnp.where(core == 0, after, incoming)
    last = pltpu.make_async_remote_copy(
        src_ref=last_out,
        dst_ref=last_in,
        send_sem=p_send.at[1],
        recv_sem=p_recv.at[1],
        device_id=partner,
        device_id_type=MESH,
    )
    last.start()

    def finish(h, rate, state):
        cols = pl.ds(pl.multiple_of(h * DH, DH), DH)
        gain = gain_ref[:, cols]
        fac = qfac[h]

        def step(b, carry):
            rows = pl.ds(pl.multiple_of(b * BLOCK, BLOCK), BLOCK)
            lift = decay(rate, BLOCK * b.astype(F32))
            prior = (before[h, b] + lift * state).astype(BF16)
            qdec = (qb[rows, cols].astype(F32) * fac).astype(BF16)
            o = intra[rows, cols] + nn(qdec, prior)
            scale = lax.rsqrt(jnp.mean(o * o, axis=-1, keepdims=True) + 1e-05)
            out_ref[rows, cols] = (o * scale * gain).astype(BF16)
            return carry

        lax.fori_loop(0, nblk, step, 0)

    finish(core, rate_here, jnp.where(core == 0, incoming, after))
    last.wait_recv()
    finish(1 - core, jnp.where(core == 0, rates[1], rates[0]), last_in[...])

    for copies in z_copies:
        for copy in copies:
            copy.wait_send()
    for copy in x_copies:
        copy.wait_send()
    for d in range(1, n_y):
        y_copy(d).wait_send()
    pair.wait_send()
    last.wait_send()


def body(queries, keys, values, decay_exp, norm_gain):
    _, part, width = queries.shape
    n_z = lax.axis_size("head")
    n_seq = lax.axis_size("seq")
    n_y = n_seq // (NX * CORES)
    wide = width // n_z
    heads_here = wide // DH
    length = part * n_z
    nblk = length // BLOCK
    total = length * n_seq
    square = (DH, DH)
    out = pl.pallas_call(
        functools.partial(kernel, n_z, n_y, total),
        out_shape=jax.ShapeDtypeStruct((length, wide), BF16),
        in_specs=[pl.BlockSpec(memory_space=pltpu.HBM)] * 3
        + [pl.BlockSpec(memory_space=pltpu.SMEM), pl.BlockSpec(memory_space=pltpu.VMEM)],
        out_specs=pl.BlockSpec(memory_space=pltpu.VMEM),
        scratch_shapes=[
            pltpu.VMEM((length, wide), BF16),
            pltpu.VMEM((length, wide), BF16),
            pltpu.VMEM((length, wide), BF16),
            pltpu.VMEM((heads_here, nblk) + square, F32),
            pltpu.VMEM((length, wide), F32),
            pltpu.VMEM((heads_here,) + square, F32),
            pltpu.VMEM((heads_here,) + square, F32),
            pltpu.VMEM((heads_here,) + square, F32),
            pltpu.VMEM((heads_here,) + square, F32),
            pltpu.VMEM(square, F32),
            pltpu.VMEM((NX,) + square, BF16),
            pltpu.VMEM((n_y,) + square, BF16),
            pltpu.VMEM(square, F32),
            pltpu.VMEM(square, F32),
            pltpu.SemaphoreType.DMA((3,)),
            pltpu.SemaphoreType.DMA((3, n_z)),
            pltpu.SemaphoreType.DMA((3, n_z)),
            pltpu.SemaphoreType.DMA((NX,)),
            pltpu.SemaphoreType.DMA((NX,)),
            pltpu.SemaphoreType.DMA((n_y,)),
            pltpu.SemaphoreType.DMA((n_y,)),
            pltpu.SemaphoreType.DMA((2,)),
            pltpu.SemaphoreType.DMA((2,)),
        ],
        compiler_params=pltpu.CompilerParams(collective_id=0, has_side_effects=True),
    )(
        queries.reshape(part, width),
        keys.reshape(part, width),
        values.reshape(part, width),
        decay_exp,
        norm_gain.reshape(1, wide),
    )
    return out.reshape(1, length, wide)


def solution(mesh):
    return jax.shard_map(
        body,
        mesh=mesh,
        in_specs=(
            P(None, ("seq", "head"), None),
            P(None, ("seq", "head"), None),
            P(None, ("seq", "head"), None),
            P(),
            P("head"),
        ),
        out_specs=P(None, "seq", "head"),
        check_vma=False,
    )
```

```python
import functools

import jax
import jax.numpy as jnp
from jax import lax
from jax.experimental import pallas as pl
from jax.experimental.pallas import tpu as pltpu
from jax.sharding import PartitionSpec as P

HEADS = 16
DH = 128
NX = 8
CORES = 2
MESH = pl.DeviceIdType.MESH
F32 = jnp.float32
BF16 = jnp.bfloat16


def power_of_two(e):
    r = jnp.float32(1.0)
    for bit in range(4):
        r = r * jnp.where((e >> bit) & 1 == 1, jnp.float32(2.0 ** (2**bit)), jnp.float32(1.0))
    return r


def nt(a, b):
    return lax.dot_general(a, b, (((1,), (1,)), ((), ())), preferred_element_type=F32)


def tn(a, b):
    return lax.dot_general(a, b, (((0,), (0,)), ((), ())), preferred_element_type=F32)


def nn(a, b):
    return jnp.dot(a, b, preferred_element_type=F32)


def kernel(
    n_z,
    n_y,
    total,
    q_hbm,
    k_hbm,
    v_hbm,
    dec_ref,
    gain_ref,
    out_ref,
    qf,
    kf,
    vf,
    state_out,
    state_in,
    intra_out,
    intra_in,
    q_in,
    near,
    fall,
    gbuf,
    pair_in,
    xbuf,
    ybuf,
    last_out,
    last_in,
    local_sem,
    z_send,
    z_recv,
    x_send,
    x_recv,
    y_send,
    y_recv,
    p_send,
    p_recv,
):
    s = lax.axis_index("seq")
    z = lax.axis_index("head")
    core = lax.rem(s, CORES)
    x = lax.rem(lax.div(s, CORES), NX)
    y = lax.div(s, CORES * NX)
    part = q_hbm.shape[0]
    wide = q_hbm.shape[1] // n_z
    length = part * n_z
    heads_here = wide // DH

    def seq_of(yy, xx, cc):
        return (yy * NX + xx) * CORES + cc

    def at_z(d):
        return (s, lax.rem(z + d, n_z))

    def at_x(d):
        return (seq_of(y, lax.rem(x + d, NX), core), z)

    def at_y(d):
        return (seq_of(lax.rem(y + d, n_y), x, core), z)

    partner = (seq_of(y, x, 1 - core), z)

    own_cols = pl.ds(pl.multiple_of(z * wide, wide), wide)
    own_rows = pl.ds(pl.multiple_of(z * part, part), part)
    loads = []
    for a, (src, dst) in enumerate(
        ((k_hbm, kf), (v_hbm, vf), (q_hbm, qf), (q_hbm.at[:, own_cols], q_in.at[own_rows]))
    ):
        copy = pltpu.make_async_copy(src, dst, local_sem.at[a])
        copy.start()
        loads.append(copy)

    barrier = pltpu.get_barrier_semaphore()
    for d in range(1, n_z):
        pl.semaphore_signal(barrier, inc=1, device_id=at_z(d), device_id_type=MESH)
    for d in range(1, NX):
        pl.semaphore_signal(barrier, inc=1, device_id=at_x(d), device_id_type=MESH)
    for d in range(1, n_y):
        pl.semaphore_signal(barrier, inc=1, device_id=at_y(d), device_id_type=MESH)
    pl.semaphore_signal(barrier, inc=1, device_id=partner, device_id_type=MESH)

    order = sorted(range(1, n_z), key=lambda d: (-min(d, n_z - d), d))

    def rate_of(head):
        return power_of_two(dec_ref[head]) / jnp.float32(2.0 * total)

    def decay(rate, tokens):
        return jnp.exp(jnp.full((1, DH), -rate * tokens, F32))

    place = lax.broadcasted_iota(jnp.int32, (part, DH), 0).astype(F32)
    loads[0].wait()
    loads[1].wait()
    for d in order + [0]:
        to = lax.rem(z + d, n_z)
        for h in range(heads_here):
            head = to * heads_here + h
            cols = pl.ds(pl.multiple_of(head * DH, DH), DH)
            rate = rate_of(head)
            grown = vf[:, cols].astype(F32) * jnp.exp(rate * (place + 1.0))
            high = grown.astype(BF16)
            low = (grown - high.astype(F32)).astype(BF16)
            both = tn(kf[:, cols], jnp.concatenate([high, low], axis=1))
            state = (both[:, :DH] + both[:, DH:]) * decay(rate, part)
            state_out[to, h] = state.astype(BF16)

    pl.semaphore_wait(barrier, n_z + NX + n_y - 2)

    def z_copy(a, d):
        to = lax.rem(z + d, n_z)
        if a == 0:
            src, dst = state_out.at[to], state_in.at[z]
        elif a == 1:
            src, dst = q_hbm.at[:, pl.ds(pl.multiple_of(to * wide, wide), wide)], q_in.at[own_rows]
        else:
            src, dst = intra_out.at[to], intra_in.at[own_rows]
        return pltpu.make_async_remote_copy(
            src_ref=src,
            dst_ref=dst,
            send_sem=z_send.at[a, d],
            recv_sem=z_recv.at[a, d],
            device_id=(s, to),
            device_id_type=MESH,
        )

    for a in (0, 1):
        for d in order:
            z_copy(a, d).start()
    own_state = pltpu.make_async_copy(state_out.at[z], state_in.at[z], local_sem.at[4])
    own_state.start()

    loads[2].wait()
    row = lax.broadcasted_iota(jnp.int32, (part, part), 0)
    col = lax.broadcasted_iota(jnp.int32, (part, part), 1)
    causal = col <= row
    key_place = lax.broadcasted_iota(jnp.int32, (1, part), 1).astype(F32)
    for d in order + [0]:
        to = lax.rem(z + d, n_z)
        for h in range(heads_here):
            head = to * heads_here + h
            cols = pl.ds(pl.multiple_of(head * DH, DH), DH)
            rise = jnp.exp(rate_of(head) * (key_place + 1.0))
            scores = nt(qf[:, cols], kf[:, cols])
            probs = jnp.where(causal, scores * rise, 0.0).astype(BF16)
            intra_out[to, :, h * DH : (h + 1) * DH] = nn(probs, vf[:, cols]).astype(BF16)
        if d:
            z_copy(2, d).start()
    own_intra = pltpu.make_async_copy(intra_out.at[z], intra_in.at[own_rows], local_sem.at[5])
    own_intra.start()

    rates = [rate_of(z * heads_here + h) for h in range(heads_here)]
    rate_here = jnp.where(core == 0, rates[0], rates[1])
    rate_other = jnp.where(core == 0, rates[1], rates[0])
    for h in range(heads_here):
        fall[h] = jnp.exp(-rates[h] * (place + 1.0))
    chip = CORES * length
    place = lax.broadcasted_iota(jnp.int32, (NX, DH), 0)
    gap = jnp.maximum(x - 1 - place, 0).astype(F32)
    x_coef = jnp.where(place < x, jnp.exp(-rate_here * (chip * gap)), 0.0)
    all_coef = jnp.exp(-rate_here * (chip * (NX - 1 - place).astype(F32)))
    place = lax.broadcasted_iota(jnp.int32, (n_y, DH), 0)
    gap = jnp.maximum(NX * (y - 1 - place) + x, 0).astype(F32)
    y_coef = jnp.where(place < y, jnp.exp(-rate_here * (chip * gap)), 0.0)
    w1 = decay(rate_here, length)

    own_state.wait()
    for d in order:
        z_copy(0, d).wait_recv()
    for h in range(heads_here):
        step_decay = decay(rates[h], part)
        group = state_in[0, h].astype(F32)
        for i in range(1, n_z):
            group = group * step_decay + state_in[i, h].astype(F32)
        gbuf[h] = group

    pair = pltpu.make_async_remote_copy(
        src_ref=gbuf.at[1 - core],
        dst_ref=pair_in,
        send_sem=p_send.at[0],
        recv_sem=p_recv.at[0],
        device_id=partner,
        device_id_type=MESH,
    )
    pair.start()
    pair.wait_recv()
    mine = gbuf[core]
    theirs = pair_in[...]
    first = jnp.where(core == 0, mine, theirs)
    second = jnp.where(core == 0, theirs, mine)
    xbuf[x] = (first * w1 + second).astype(BF16)
    x_copies = []
    for d in range(1, NX):
        copy = pltpu.make_async_remote_copy(
            src_ref=xbuf.at[x],
            dst_ref=xbuf.at[x],
            send_sem=x_send.at[d],
            recv_sem=x_recv.at[d],
            device_id=at_x(d),
            device_id_type=MESH,
        )
        copy.start()
        x_copies.append(copy)
    for copy in x_copies:
        copy.wait_recv()
    in_row = jnp.zeros((DH, DH), F32)
    row_total = jnp.zeros((DH, DH), F32)
    for i in range(NX):
        state = xbuf[i].astype(F32)
        in_row += state * x_coef[i : i + 1]
        row_total += state * all_coef[i : i + 1]
    ybuf[y] = row_total.astype(BF16)

    def y_copy(d):
        return pltpu.make_async_remote_copy(
            src_ref=ybuf.at[y],
            dst_ref=ybuf.at[y],
            send_sem=y_send.at[d],
            recv_sem=y_recv.at[d],
            device_id=at_y(d),
            device_id_type=MESH,
        )

    for d in range(1, n_y):
        y_copy(d).start()
    for d in range(1, n_y):
        y_copy(d).wait_recv()
    incoming = in_row
    for i in range(n_y):
        incoming += ybuf[i].astype(F32) * y_coef[i : i + 1]
    after = incoming * w1 + first
    last_out[...] = jnp.where(core == 0, after, incoming)
    last = pltpu.make_async_remote_copy(
        src_ref=last_out,
        dst_ref=last_in,
        send_sem=p_send.at[1],
        recv_sem=p_recv.at[1],
        device_id=partner,
        device_id_type=MESH,
    )
    last.start()

    loads[3].wait()
    for d in order:
        z_copy(1, d).wait_recv()

    def earlier(h, rate, state):
        cols = pl.ds(pl.multiple_of(h * DH, DH), DH)
        step_decay = decay(rate, part)
        for i in range(n_z):
            rows = slice(i * part, (i + 1) * part)
            high = state.astype(BF16)
            low = (state - high.astype(F32)).astype(BF16)
            query = q_in[rows, cols]
            near[h, rows] = nn(
                jnp.concatenate([query, query], axis=1), jnp.concatenate([high, low], axis=0)
            )
            if i < n_z - 1:
                state = state * step_decay + state_in[i, h].astype(F32)

    earlier(core, rate_here, jnp.where(core == 0, incoming, after))
    last.wait_recv()
    earlier(1 - core, rate_other, last_in[...])

    for d in [0] + order:
        if d:
            z_copy(2, d).wait_recv()
        else:
            own_intra.wait()
        src = lax.rem(z + n_z - d, n_z)
        rows = pl.ds(pl.multiple_of(src * part, part), part)
        for h in range(heads_here):
            cols = slice(h * DH, (h + 1) * DH)
            o = (near[h, rows] + intra_in[rows, cols].astype(F32)) * fall[h]
            scale = lax.rsqrt(jnp.mean(o * o, axis=-1, keepdims=True) + 1e-05)
            out_ref[rows, cols] = (o * scale * gain_ref[:, cols]).astype(BF16)

    for a in range(3):
        for d in order:
            z_copy(a, d).wait_send()
    for copy in x_copies:
        copy.wait_send()
    for d in range(1, n_y):
        y_copy(d).wait_send()
    pair.wait_send()
    last.wait_send()


def body(queries, keys, values, decay_exp, norm_gain):
    _, part, width = queries.shape
    n_z = lax.axis_size("head")
    n_seq = lax.axis_size("seq")
    n_y = n_seq // (NX * CORES)
    wide = width // n_z
    heads_here = wide // DH
    length = part * n_z
    total = length * n_seq
    square = (DH, DH)
    out = pl.pallas_call(
        functools.partial(kernel, n_z, n_y, total),
        out_shape=jax.ShapeDtypeStruct((length, wide), BF16),
        in_specs=[pl.BlockSpec(memory_space=pltpu.HBM)] * 3
        + [pl.BlockSpec(memory_space=pltpu.SMEM), pl.BlockSpec(memory_space=pltpu.VMEM)],
        out_specs=pl.BlockSpec(memory_space=pltpu.VMEM),
        scratch_shapes=[
            pltpu.VMEM((part, width), BF16),
            pltpu.VMEM((part, width), BF16),
            pltpu.VMEM((part, width), BF16),
            pltpu.VMEM((n_z, heads_here) + square, BF16),
            pltpu.VMEM((n_z, heads_here) + square, BF16),
            pltpu.VMEM((n_z, part, wide), BF16),
            pltpu.VMEM((length, wide), BF16),
            pltpu.VMEM((length, wide), BF16),
            pltpu.VMEM((heads_here, length, DH), F32),
            pltpu.VMEM((heads_here, part, DH), F32),
            pltpu.VMEM((heads_here,) + square, F32),
            pltpu.VMEM(square, F32),
            pltpu.VMEM((NX,) + square, BF16),
            pltpu.VMEM((n_y,) + square, BF16),
            pltpu.VMEM(square, F32),
            pltpu.VMEM(square, F32),
            pltpu.SemaphoreType.DMA((6,)),
            pltpu.SemaphoreType.DMA((3, n_z)),
            pltpu.SemaphoreType.DMA((3, n_z)),
            pltpu.SemaphoreType.DMA((NX,)),
            pltpu.SemaphoreType.DMA((NX,)),
            pltpu.SemaphoreType.DMA((n_y,)),
            pltpu.SemaphoreType.DMA((n_y,)),
            pltpu.SemaphoreType.DMA((2,)),
            pltpu.SemaphoreType.DMA((2,)),
        ],
        compiler_params=pltpu.CompilerParams(collective_id=0, has_side_effects=True),
    )(
        queries.reshape(part, width),
        keys.reshape(part, width),
        values.reshape(part, width),
        decay_exp,
        norm_gain.reshape(1, wide),
    )
    return out.reshape(1, length, wide)


def solution(mesh):
    return jax.shard_map(
        body,
        mesh=mesh,
        in_specs=(
            P(None, ("seq", "head"), None),
            P(None, ("seq", "head"), None),
            P(None, ("seq", "head"), None),
            P(),
            P("head"),
        ),
        out_specs=P(None, "seq", "head"),
        check_vma=False,
    )
```

```python
import functools

import jax
import jax.numpy as jnp
from jax import lax
from jax.experimental import pallas as pl
from jax.experimental.pallas import tpu as pltpu
from jax.sharding import PartitionSpec as P

HEADS = 16
DH = 128
NX = 8
CORES = 2
MESH = pl.DeviceIdType.MESH
F32 = jnp.float32
BF16 = jnp.bfloat16


def power_of_two(e):
    r = jnp.float32(1.0)
    for bit in range(4):
        r = r * jnp.where((e >> bit) & 1 == 1, jnp.float32(2.0 ** (2**bit)), jnp.float32(1.0))
    return r


def nt(a, b):
    return lax.dot_general(a, b, (((1,), (1,)), ((), ())), preferred_element_type=F32)


def tn(a, b):
    return lax.dot_general(a, b, (((0,), (0,)), ((), ())), preferred_element_type=F32)


def nn(a, b):
    return jnp.dot(a, b, preferred_element_type=F32)


def kernel(
    n_z,
    n_y,
    total,
    q_hbm,
    k_hbm,
    v_hbm,
    dec_hbm,
    gain_hbm,
    out_ref,
    dec_ref,
    gain_ref,
    qf,
    kf,
    vf,
    state_out,
    state_in,
    intra_out,
    intra_in,
    q_in,
    near,
    fall,
    gbuf,
    pair_in,
    xbuf,
    ybuf,
    last_out,
    last_in,
    local_sem,
    z_send,
    z_recv,
    x_send,
    x_recv,
    y_send,
    y_recv,
    p_send,
    p_recv,
):
    s = lax.axis_index("seq")
    z = lax.axis_index("head")
    core = lax.rem(s, CORES)
    x = lax.rem(lax.div(s, CORES), NX)
    y = lax.div(s, CORES * NX)
    part = q_hbm.shape[0]
    wide = q_hbm.shape[1] // n_z
    length = part * n_z
    heads_here = wide // DH

    def seq_of(yy, xx, cc):
        return (yy * NX + xx) * CORES + cc

    def at_z(d):
        return (s, lax.rem(z + d, n_z))

    def at_x(d):
        return (seq_of(y, lax.rem(x + d, NX), core), z)

    def at_y(d):
        return (seq_of(lax.rem(y + d, n_y), x, core), z)

    partner = (seq_of(y, x, 1 - core), z)

    barrier = pltpu.get_barrier_semaphore()
    for d in range(1, n_z):
        pl.semaphore_signal(barrier, inc=1, device_id=at_z(d), device_id_type=MESH)
    for d in range(1, NX):
        pl.semaphore_signal(barrier, inc=1, device_id=at_x(d), device_id_type=MESH)
    for d in range(1, n_y):
        pl.semaphore_signal(barrier, inc=1, device_id=at_y(d), device_id_type=MESH)
    pl.semaphore_signal(barrier, inc=1, device_id=partner, device_id_type=MESH)

    own_cols = pl.ds(pl.multiple_of(z * wide, wide), wide)
    own_rows = pl.ds(pl.multiple_of(z * part, part), part)
    loads = []
    for a, (src, dst) in enumerate(
        (
            (k_hbm, kf),
            (v_hbm, vf),
            (q_hbm, qf),
            (q_hbm.at[:, own_cols], q_in.at[own_rows]),
            (dec_hbm, dec_ref),
            (gain_hbm, gain_ref),
        )
    ):
        copy = pltpu.make_async_copy(src, dst, local_sem.at[a])
        copy.start()
        loads.append(copy)

    order = sorted(range(1, n_z), key=lambda d: (-min(d, n_z - d), d))

    def rate_of(head):
        return power_of_two(dec_ref[head]) / jnp.float32(2.0 * total)

    def decay(rate, tokens):
        return jnp.exp(jnp.full((1, DH), -rate * tokens, F32))

    place = lax.broadcasted_iota(jnp.int32, (part, DH), 0).astype(F32)
    loads[4].wait()
    loads[0].wait()
    loads[1].wait()
    for d in order + [0]:
        to = lax.rem(z + d, n_z)
        for h in range(heads_here):
            head = to * heads_here + h
            cols = pl.ds(pl.multiple_of(head * DH, DH), DH)
            rate = rate_of(head)
            grown = vf[:, cols].astype(F32) * jnp.exp(rate * (place + 1.0))
            high = grown.astype(BF16)
            low = (grown - high.astype(F32)).astype(BF16)
            both = tn(kf[:, cols], jnp.concatenate([high, low], axis=1))
            state = (both[:, :DH] + both[:, DH:]) * decay(rate, part)
            state_out[to, h] = state.astype(BF16)

    pl.semaphore_wait(barrier, n_z + NX + n_y - 2)

    def z_copy(a, d):
        to = lax.rem(z + d, n_z)
        if a == 0:
            src, dst = state_out.at[to], state_in.at[z]
        elif a == 1:
            src, dst = q_hbm.at[:, pl.ds(pl.multiple_of(to * wide, wide), wide)], q_in.at[own_rows]
        else:
            src, dst = intra_out.at[to], intra_in.at[own_rows]
        return pltpu.make_async_remote_copy(
            src_ref=src,
            dst_ref=dst,
            send_sem=z_send.at[a, d],
            recv_sem=z_recv.at[a, d],
            device_id=(s, to),
            device_id_type=MESH,
        )

    for a in (0, 1):
        for d in order:
            z_copy(a, d).start()
    own_state = pltpu.make_async_copy(state_out.at[z], state_in.at[z], local_sem.at[6])
    own_state.start()

    loads[2].wait()
    row = lax.broadcasted_iota(jnp.int32, (part, part), 0)
    col = lax.broadcasted_iota(jnp.int32, (part, part), 1)
    causal = col <= row
    key_place = lax.broadcasted_iota(jnp.int32, (1, part), 1).astype(F32)
    for d in order + [0]:
        to = lax.rem(z + d, n_z)
        for h in range(heads_here):
            head = to * heads_here + h
            cols = pl.ds(pl.multiple_of(head * DH, DH), DH)
            rise = jnp.exp(rate_of(head) * (key_place + 1.0))
            scores = nt(qf[:, cols], kf[:, cols])
            probs = jnp.where(causal, scores * rise, 0.0).astype(BF16)
            intra_out[to, :, h * DH : (h + 1) * DH] = nn(probs, vf[:, cols]).astype(BF16)
        if d:
            z_copy(2, d).start()
    own_intra = pltpu.make_async_copy(intra_out.at[z], intra_in.at[own_rows], local_sem.at[7])
    own_intra.start()

    rates = [rate_of(z * heads_here + h) for h in range(heads_here)]
    rate_here = jnp.where(core == 0, rates[0], rates[1])
    rate_other = jnp.where(core == 0, rates[1], rates[0])
    for h in range(heads_here):
        fall[h] = jnp.exp(-rates[h] * (place + 1.0))
    chip = CORES * length
    place = lax.broadcasted_iota(jnp.int32, (NX, DH), 0)
    gap = jnp.maximum(x - 1 - place, 0).astype(F32)
    x_coef = jnp.where(place < x, jnp.exp(-rate_here * (chip * gap)), 0.0)
    all_coef = jnp.exp(-rate_here * (chip * (NX - 1 - place).astype(F32)))
    place = lax.broadcasted_iota(jnp.int32, (n_y, DH), 0)
    gap = jnp.maximum(NX * (y - 1 - place) + x, 0).astype(F32)
    y_coef = jnp.where(place < y, jnp.exp(-rate_here * (chip * gap)), 0.0)
    w1 = decay(rate_here, length)

    own_state.wait()
    for d in order:
        z_copy(0, d).wait_recv()
    for h in range(heads_here):
        step_decay = decay(rates[h], part)
        group = state_in[0, h].astype(F32)
        for i in range(1, n_z):
            group = group * step_decay + state_in[i, h].astype(F32)
        gbuf[h] = group

    pair = pltpu.make_async_remote_copy(
        src_ref=gbuf.at[1 - core],
        dst_ref=pair_in,
        send_sem=p_send.at[0],
        recv_sem=p_recv.at[0],
        device_id=partner,
        device_id_type=MESH,
    )
    pair.start()
    pair.wait_recv()
    mine = gbuf[core]
    theirs = pair_in[...]
    first = jnp.where(core == 0, mine, theirs)
    second = jnp.where(core == 0, theirs, mine)
    xbuf[x] = (first * w1 + second).astype(BF16)
    x_copies = []
    for d in range(1, NX):
        copy = pltpu.make_async_remote_copy(
            src_ref=xbuf.at[x],
            dst_ref=xbuf.at[x],
            send_sem=x_send.at[d],
            recv_sem=x_recv.at[d],
            device_id=at_x(d),
            device_id_type=MESH,
        )
        copy.start()
        x_copies.append(copy)
    for copy in x_copies:
        copy.wait_recv()
    in_row = jnp.zeros((DH, DH), F32)
    row_total = jnp.zeros((DH, DH), F32)
    for i in range(NX):
        state = xbuf[i].astype(F32)
        in_row += state * x_coef[i : i + 1]
        row_total += state * all_coef[i : i + 1]
    ybuf[y] = row_total.astype(BF16)

    def y_copy(d):
        return pltpu.make_async_remote_copy(
            src_ref=ybuf.at[y],
            dst_ref=ybuf.at[y],
            send_sem=y_send.at[d],
            recv_sem=y_recv.at[d],
            device_id=at_y(d),
            device_id_type=MESH,
        )

    for d in range(1, n_y):
        y_copy(d).start()
    for d in range(1, n_y):
        y_copy(d).wait_recv()
    incoming = in_row
    for i in range(n_y):
        incoming += ybuf[i].astype(F32) * y_coef[i : i + 1]
    after = incoming * w1 + first
    last_out[...] = jnp.where(core == 0, after, incoming)
    last = pltpu.make_async_remote_copy(
        src_ref=last_out,
        dst_ref=last_in,
        send_sem=p_send.at[1],
        recv_sem=p_recv.at[1],
        device_id=partner,
        device_id_type=MESH,
    )
    last.start()

    loads[3].wait()
    loads[5].wait()
    for d in order:
        z_copy(1, d).wait_recv()

    def earlier(h, rate, state):
        cols = pl.ds(pl.multiple_of(h * DH, DH), DH)
        step_decay = decay(rate, part)
        for i in range(n_z):
            rows = slice(i * part, (i + 1) * part)
            high = state.astype(BF16)
            low = (state - high.astype(F32)).astype(BF16)
            query = q_in[rows, cols]
            near[h, rows] = nn(
                jnp.concatenate([query, query], axis=1), jnp.concatenate([high, low], axis=0)
            )
            if i < n_z - 1:
                state = state * step_decay + state_in[i, h].astype(F32)

    earlier(core, rate_here, jnp.where(core == 0, incoming, after))
    last.wait_recv()
    earlier(1 - core, rate_other, last_in[...])

    for d in [0] + order:
        if d:
            z_copy(2, d).wait_recv()
        else:
            own_intra.wait()
        src = lax.rem(z + n_z - d, n_z)
        rows = pl.ds(pl.multiple_of(src * part, part), part)
        for h in range(heads_here):
            cols = slice(h * DH, (h + 1) * DH)
            o = (near[h, rows] + intra_in[rows, cols].astype(F32)) * fall[h]
            scale = lax.rsqrt(jnp.mean(o * o, axis=-1, keepdims=True) + 1e-05)
            out_ref[rows, cols] = (o * scale * gain_ref[:, cols]).astype(BF16)

    for a in range(3):
        for d in order:
            z_copy(a, d).wait_send()
    for copy in x_copies:
        copy.wait_send()
    for d in range(1, n_y):
        y_copy(d).wait_send()
    pair.wait_send()
    last.wait_send()


def body(queries, keys, values, decay_exp, norm_gain):
    _, part, width = queries.shape
    n_z = lax.axis_size("head")
    n_seq = lax.axis_size("seq")
    n_y = n_seq // (NX * CORES)
    wide = width // n_z
    heads_here = wide // DH
    length = part * n_z
    total = length * n_seq
    square = (DH, DH)
    heads = decay_exp.shape[0]
    out = pl.pallas_call(
        functools.partial(kernel, n_z, n_y, total),
        out_shape=pltpu.VMEM((length, wide), BF16),
        in_specs=[pl.BlockSpec(memory_space=pltpu.HBM)] * 5,
        out_specs=pl.BlockSpec(memory_space=pltpu.VMEM),
        scratch_shapes=[
            pltpu.SMEM((heads,), jnp.int32),
            pltpu.VMEM((1, wide), F32),
            pltpu.VMEM((part, width), BF16),
            pltpu.VMEM((part, width), BF16),
            pltpu.VMEM((part, width), BF16),
            pltpu.VMEM((n_z, heads_here) + square, BF16),
            pltpu.VMEM((n_z, heads_here) + square, BF16),
            pltpu.VMEM((n_z, part, wide), BF16),
            pltpu.VMEM((length, wide), BF16),
            pltpu.VMEM((length, wide), BF16),
            pltpu.VMEM((heads_here, length, DH), F32),
            pltpu.VMEM((heads_here, part, DH), F32),
            pltpu.VMEM((heads_here,) + square, F32),
            pltpu.VMEM(square, F32),
            pltpu.VMEM((NX,) + square, BF16),
            pltpu.VMEM((n_y,) + square, BF16),
            pltpu.VMEM(square, F32),
            pltpu.VMEM(square, F32),
            pltpu.SemaphoreType.DMA((8,)),
            pltpu.SemaphoreType.DMA((3, n_z)),
            pltpu.SemaphoreType.DMA((3, n_z)),
            pltpu.SemaphoreType.DMA((NX,)),
            pltpu.SemaphoreType.DMA((NX,)),
            pltpu.SemaphoreType.DMA((n_y,)),
            pltpu.SemaphoreType.DMA((n_y,)),
            pltpu.SemaphoreType.DMA((2,)),
            pltpu.SemaphoreType.DMA((2,)),
        ],
        compiler_params=pltpu.CompilerParams(collective_id=0, has_side_effects=True),
    )(
        queries.reshape(part, width),
        keys.reshape(part, width),
        values.reshape(part, width),
        decay_exp,
        norm_gain.reshape(1, wide),
    )
    return out.reshape(1, length, wide)


def solution(mesh):
    return jax.shard_map(
        body,
        mesh=mesh,
        in_specs=(
            P(None, ("seq", "head"), None),
            P(None, ("seq", "head"), None),
            P(None, ("seq", "head"), None),
            P(),
            P("head"),
        ),
        out_specs=P(None, "seq", "head"),
        check_vma=False,
    )
```

```python
import functools

import jax
import jax.numpy as jnp
from jax import lax
from jax.experimental import pallas as pl
from jax.experimental.pallas import tpu as pltpu
from jax.sharding import PartitionSpec as P

HEADS = 16
DH = 128
NX = 8
CORES = 2
MESH = pl.DeviceIdType.MESH
F32 = jnp.float32
BF16 = jnp.bfloat16


def power_of_two(e):
    r = jnp.float32(1.0)
    for bit in range(4):
        r = r * jnp.where((e >> bit) & 1 == 1, jnp.float32(2.0 ** (2**bit)), jnp.float32(1.0))
    return r


def nt(a, b):
    return lax.dot_general(a, b, (((1,), (1,)), ((), ())), preferred_element_type=F32)


def tn(a, b):
    return lax.dot_general(a, b, (((0,), (0,)), ((), ())), preferred_element_type=F32)


def nn(a, b):
    return jnp.dot(a, b, preferred_element_type=F32)


def kernel(
    n_z,
    n_y,
    total,
    q_hbm,
    k_hbm,
    v_hbm,
    dec_hbm,
    gain_hbm,
    out_ref,
    dec_ref,
    gain_ref,
    qf,
    kf,
    vf,
    state_out,
    state_in,
    intra_out,
    intra_in,
    q_in,
    near,
    fall,
    gbuf,
    pair_in,
    xbuf,
    ybuf,
    last_out,
    last_in,
    local_sem,
    z_send,
    z_recv,
    x_send,
    x_recv,
    y_send,
    y_recv,
    p_send,
    p_recv,
):
    s = lax.axis_index("seq")
    z = lax.axis_index("head")
    core = lax.rem(s, CORES)
    x = lax.rem(lax.div(s, CORES), NX)
    y = lax.div(s, CORES * NX)
    part = q_hbm.shape[0]
    wide = q_hbm.shape[1] // n_z
    length = part * n_z
    heads_here = wide // DH

    def seq_of(yy, xx, cc):
        return (yy * NX + xx) * CORES + cc

    def at_z(d):
        return (s, lax.rem(z + d, n_z))

    def at_x(d):
        return (seq_of(y, lax.rem(x + d, NX), core), z)

    def at_y(d):
        return (seq_of(lax.rem(y + d, n_y), x, core), z)

    partner = (seq_of(y, x, 1 - core), z)

    barrier = pltpu.get_barrier_semaphore()
    for d in range(1, n_z):
        pl.semaphore_signal(barrier, inc=1, device_id=at_z(d), device_id_type=MESH)
    for d in range(1, NX):
        pl.semaphore_signal(barrier, inc=1, device_id=at_x(d), device_id_type=MESH)
    for d in range(1, n_y):
        pl.semaphore_signal(barrier, inc=1, device_id=at_y(d), device_id_type=MESH)
    pl.semaphore_signal(barrier, inc=1, device_id=partner, device_id_type=MESH)

    own_cols = pl.ds(pl.multiple_of(z * wide, wide), wide)
    own_rows = pl.ds(pl.multiple_of(z * part, part), part)
    loads = []
    for a, (src, dst) in enumerate(
        (
            (k_hbm, kf),
            (v_hbm, vf),
            (q_hbm, qf),
            (q_hbm.at[:, own_cols], q_in.at[own_rows]),
            (dec_hbm, dec_ref),
            (gain_hbm, gain_ref),
        )
    ):
        copy = pltpu.make_async_copy(src, dst, local_sem.at[a])
        copy.start()
        loads.append(copy)

    order = sorted(range(1, n_z), key=lambda d: (min(d, n_z - d), d))
    state_order = sorted(range(1, n_z), key=lambda d: (-min(d, n_z - d), d))

    def rate_of(head):
        return power_of_two(dec_ref[head]) / jnp.float32(2.0 * total)

    def decay(rate, tokens):
        return jnp.exp(jnp.full((1, DH), -rate * tokens, F32))

    place = lax.broadcasted_iota(jnp.int32, (part, DH), 0).astype(F32)
    loads[4].wait()
    loads[0].wait()
    loads[1].wait()
    for d in order + [0]:
        to = lax.rem(z + d, n_z)
        for h in range(heads_here):
            head = to * heads_here + h
            cols = pl.ds(pl.multiple_of(head * DH, DH), DH)
            rate = rate_of(head)
            grown = vf[:, cols].astype(F32) * jnp.exp(rate * (place + 1.0))
            high = grown.astype(BF16)
            low = (grown - high.astype(F32)).astype(BF16)
            both = tn(kf[:, cols], jnp.concatenate([high, low], axis=1))
            state = (both[:, :DH] + both[:, DH:]) * decay(rate, part)
            state_out[to, h] = state.astype(BF16)

    pl.semaphore_wait(barrier, n_z + NX + n_y - 2)

    def z_copy(a, d):
        to = lax.rem(z + d, n_z)
        if a == 0:
            src, dst = state_out.at[to], state_in.at[z]
        elif a == 1:
            src, dst = q_hbm.at[:, pl.ds(pl.multiple_of(to * wide, wide), wide)], q_in.at[own_rows]
        else:
            src, dst = intra_out.at[to], intra_in.at[own_rows]
        return pltpu.make_async_remote_copy(
            src_ref=src,
            dst_ref=dst,
            send_sem=z_send.at[a, d],
            recv_sem=z_recv.at[a, d],
            device_id=(s, to),
            device_id_type=MESH,
        )

    for d in state_order:
        z_copy(0, d).start()
    for d in order:
        z_copy(1, d).start()
    own_state = pltpu.make_async_copy(state_out.at[z], state_in.at[z], local_sem.at[6])
    own_state.start()

    loads[2].wait()
    row = lax.broadcasted_iota(jnp.int32, (part, part), 0)
    col = lax.broadcasted_iota(jnp.int32, (part, part), 1)
    causal = col <= row
    key_place = lax.broadcasted_iota(jnp.int32, (1, part), 1).astype(F32)
    for d in order + [0]:
        to = lax.rem(z + d, n_z)
        for h in range(heads_here):
            head = to * heads_here + h
            cols = pl.ds(pl.multiple_of(head * DH, DH), DH)
            rise = jnp.exp(rate_of(head) * (key_place + 1.0))
            scores = nt(qf[:, cols], kf[:, cols])
            probs = jnp.where(causal, scores * rise, 0.0).astype(BF16)
            intra_out[to, :, h * DH : (h + 1) * DH] = nn(probs, vf[:, cols]).astype(BF16)
        if d:
            z_copy(2, d).start()
    own_intra = pltpu.make_async_copy(intra_out.at[z], intra_in.at[own_rows], local_sem.at[7])
    own_intra.start()

    rates = [rate_of(z * heads_here + h) for h in range(heads_here)]
    rate_here = jnp.where(core == 0, rates[0], rates[1])
    rate_other = jnp.where(core == 0, rates[1], rates[0])
    for h in range(heads_here):
        fall[h] = jnp.exp(-rates[h] * (place + 1.0))
    chip = CORES * length
    place = lax.broadcasted_iota(jnp.int32, (NX, DH), 0)
    gap = jnp.maximum(x - 1 - place, 0).astype(F32)
    x_coef = jnp.where(place < x, jnp.exp(-rate_here * (chip * gap)), 0.0)
    all_coef = jnp.exp(-rate_here * (chip * (NX - 1 - place).astype(F32)))
    place = lax.broadcasted_iota(jnp.int32, (n_y, DH), 0)
    gap = jnp.maximum(NX * (y - 1 - place) + x, 0).astype(F32)
    y_coef = jnp.where(place < y, jnp.exp(-rate_here * (chip * gap)), 0.0)
    w1 = decay(rate_here, length)

    own_state.wait()
    for d in order:
        z_copy(0, d).wait_recv()
    for h in range(heads_here):
        step_decay = decay(rates[h], part)
        group = state_in[0, h].astype(F32)
        for i in range(1, n_z):
            group = group * step_decay + state_in[i, h].astype(F32)
        gbuf[h] = group

    pair = pltpu.make_async_remote_copy(
        src_ref=gbuf.at[1 - core],
        dst_ref=pair_in,
        send_sem=p_send.at[0],
        recv_sem=p_recv.at[0],
        device_id=partner,
        device_id_type=MESH,
    )
    pair.start()
    pair.wait_recv()
    mine = gbuf[core]
    theirs = pair_in[...]
    first = jnp.where(core == 0, mine, theirs)
    second = jnp.where(core == 0, theirs, mine)
    xbuf[x] = (first * w1 + second).astype(BF16)
    x_copies = []
    for d in range(1, NX):
        copy = pltpu.make_async_remote_copy(
            src_ref=xbuf.at[x],
            dst_ref=xbuf.at[x],
            send_sem=x_send.at[d],
            recv_sem=x_recv.at[d],
            device_id=at_x(d),
            device_id_type=MESH,
        )
        copy.start()
        x_copies.append(copy)
    for copy in x_copies:
        copy.wait_recv()
    in_row = jnp.zeros((DH, DH), F32)
    row_total = jnp.zeros((DH, DH), F32)
    for i in range(NX):
        state = xbuf[i].astype(F32)
        in_row += state * x_coef[i : i + 1]
        row_total += state * all_coef[i : i + 1]
    ybuf[y] = row_total.astype(BF16)

    def y_copy(d):
        return pltpu.make_async_remote_copy(
            src_ref=ybuf.at[y],
            dst_ref=ybuf.at[y],
            send_sem=y_send.at[d],
            recv_sem=y_recv.at[d],
            device_id=at_y(d),
            device_id_type=MESH,
        )

    for d in range(1, n_y):
        y_copy(d).start()
    for d in range(1, n_y):
        y_copy(d).wait_recv()
    incoming = in_row
    for i in range(n_y):
        incoming += ybuf[i].astype(F32) * y_coef[i : i + 1]
    after = incoming * w1 + first
    last_out[...] = jnp.where(core == 0, after, incoming)
    last = pltpu.make_async_remote_copy(
        src_ref=last_out,
        dst_ref=last_in,
        send_sem=p_send.at[1],
        recv_sem=p_recv.at[1],
        device_id=partner,
        device_id_type=MESH,
    )
    last.start()

    loads[3].wait()
    loads[5].wait()
    for d in order:
        z_copy(1, d).wait_recv()

    def earlier(h, rate, state):
        cols = pl.ds(pl.multiple_of(h * DH, DH), DH)
        step_decay = decay(rate, part)
        for i in range(n_z):
            rows = slice(i * part, (i + 1) * part)
            high = state.astype(BF16)
            low = (state - high.astype(F32)).astype(BF16)
            query = q_in[rows, cols]
            near[h, rows] = nn(
                jnp.concatenate([query, query], axis=1), jnp.concatenate([high, low], axis=0)
            )
            if i < n_z - 1:
                state = state * step_decay + state_in[i, h].astype(F32)

    earlier(core, rate_here, jnp.where(core == 0, incoming, after))
    last.wait_recv()
    earlier(1 - core, rate_other, last_in[...])

    for d in [0] + order:
        if d:
            z_copy(2, d).wait_recv()
        else:
            own_intra.wait()
        src = lax.rem(z + n_z - d, n_z)
        rows = pl.ds(pl.multiple_of(src * part, part), part)
        for h in range(heads_here):
            cols = slice(h * DH, (h + 1) * DH)
            o = (near[h, rows] + intra_in[rows, cols].astype(F32)) * fall[h]
            scale = lax.rsqrt(jnp.mean(o * o, axis=-1, keepdims=True) + 1e-05)
            out_ref[rows, cols] = (o * scale * gain_ref[:, cols]).astype(BF16)

    for a in range(3):
        for d in order:
            z_copy(a, d).wait_send()
    for copy in x_copies:
        copy.wait_send()
    for d in range(1, n_y):
        y_copy(d).wait_send()
    pair.wait_send()
    last.wait_send()


def body(queries, keys, values, decay_exp, norm_gain):
    _, part, width = queries.shape
    n_z = lax.axis_size("head")
    n_seq = lax.axis_size("seq")
    n_y = n_seq // (NX * CORES)
    wide = width // n_z
    heads_here = wide // DH
    length = part * n_z
    total = length * n_seq
    square = (DH, DH)
    heads = decay_exp.shape[0]
    out = pl.pallas_call(
        functools.partial(kernel, n_z, n_y, total),
        out_shape=pltpu.VMEM((length, wide), BF16),
        in_specs=[pl.BlockSpec(memory_space=pltpu.HBM)] * 5,
        out_specs=pl.BlockSpec(memory_space=pltpu.VMEM),
        scratch_shapes=[
            pltpu.SMEM((heads,), jnp.int32),
            pltpu.VMEM((1, wide), F32),
            pltpu.VMEM((part, width), BF16),
            pltpu.VMEM((part, width), BF16),
            pltpu.VMEM((part, width), BF16),
            pltpu.VMEM((n_z, heads_here) + square, BF16),
            pltpu.VMEM((n_z, heads_here) + square, BF16),
            pltpu.VMEM((n_z, part, wide), BF16),
            pltpu.VMEM((length, wide), BF16),
            pltpu.VMEM((length, wide), BF16),
            pltpu.VMEM((heads_here, length, DH), F32),
            pltpu.VMEM((heads_here, part, DH), F32),
            pltpu.VMEM((heads_here,) + square, F32),
            pltpu.VMEM(square, F32),
            pltpu.VMEM((NX,) + square, BF16),
            pltpu.VMEM((n_y,) + square, BF16),
            pltpu.VMEM(square, F32),
            pltpu.VMEM(square, F32),
            pltpu.SemaphoreType.DMA((8,)),
            pltpu.SemaphoreType.DMA((3, n_z)),
            pltpu.SemaphoreType.DMA((3, n_z)),
            pltpu.SemaphoreType.DMA((NX,)),
            pltpu.SemaphoreType.DMA((NX,)),
            pltpu.SemaphoreType.DMA((n_y,)),
            pltpu.SemaphoreType.DMA((n_y,)),
            pltpu.SemaphoreType.DMA((2,)),
            pltpu.SemaphoreType.DMA((2,)),
        ],
        compiler_params=pltpu.CompilerParams(collective_id=0, has_side_effects=True),
    )(
        queries.reshape(part, width),
        keys.reshape(part, width),
        values.reshape(part, width),
        decay_exp,
        norm_gain.reshape(1, wide),
    )
    return out.reshape(1, length, wide)


def solution(mesh):
    return jax.shard_map(
        body,
        mesh=mesh,
        in_specs=(
            P(None, ("seq", "head"), None),
            P(None, ("seq", "head"), None),
            P(None, ("seq", "head"), None),
            P(),
            P("head"),
        ),
        out_specs=P(None, "seq", "head"),
        check_vma=False,
    )
```
